32 devices in a mesh: groups: 2 (over x), head: 16 (over z, y, core).
Axes of the slice: x: 2, y: 2, z: 4, core: 2. Of those that a mesh axis runs over, the one named last changes fastest.
Arguments:
- queries: bfloat16 [256, 2048], P('groups', 'head'), parts along dimension 0, may hold values from -400 to 400
- cache: bfloat16 [2, 8192, 128], P(None, ('groups', 'head')), parts along dimension 1, may hold values from -5 to 5
- cache_scale: bfloat16 [2, 1, 8192], P(None, None, ('groups', 'head')), parts along dimension 2, may hold values from 0.5 to 4
- offsets: int32 [4], P('groups'), parts along dimension 0, may hold values from 0 to 2048, as said below
- lengths: int32 [4], P('groups'), parts along dimension 0, may hold values from 64 to 2048, as said below
- clamp_code: int32 [2], P('groups'), parts along dimension 0, may hold values from 512 to 1535
- w_out: bfloat16 [2048, 16384], P('head'), may hold values from -0.125 to 0.125
Outputs:
- projected: bfloat16 [16384, 256], P('head', 'groups'), parts along dimension 1
The draws below stay inside these ranges and needn't reach their ends.
There are 2 independent parts, one for each index of `groups`. The reference program is written for one: setup_inputs(seed, part) draws one part's arguments, and reference() takes and returns one part's arrays. A program takes and returns all parts, laid end to end along the dimension named above; an argument that names none is the same for every part. Nothing has to cross between parts.
Inputs may be any that keep to these rules, and one draw needn't show every extreme that they name: Request r's cache region is offsets[r] to offsets[r] + lengths[r] - 1 and lies within positions r * 2048 to (r + 1) * 2048 - 1. `lengths`: the last 64 positions of each region hold the span's own keys and values; in every draw some request's length is exactly 2048.
All inputs are finite; a program needn't handle non-finite values.
Results may differ from the reference program's by a relative error of at most 0.0068.
Values may be sent and summed in bfloat16 or wider, within the bound.
No kernel may reach another device: no remote copies, remote signals or barrier semaphores. Data moves between devices by JAX's collectives and lax.ppermute only.
A program may use at most 128 MiB of HBM per device.

```python
import math
import jax
import jax.numpy as jnp
from jax import lax

HD = 128
D = 16384
HEADS = 16
KVH = 1
REQS = 2
SPAN = 64
LEN = 4096
SEG = 2048


def layout(key):
    base_key = jax.random.fold_in(key, 7101)
    key_len, key_full, key_start = jax.random.split(base_key, 3)
    lengths = jax.random.randint(key_len, (REQS,), SPAN, SEG + 1)
    full_req = jax.random.randint(key_full, (), 0, REQS)
    req_index = jnp.arange(REQS, dtype=jnp.int32)
    lengths = jnp.where(req_index == full_req, SEG, lengths).astype(jnp.int32)
    start_shift = jax.random.randint(key_start, (REQS,), 0, 1 << 30) % (SEG - lengths + 1)
    start_shift = jnp.where(req_index == REQS - 1, 0, start_shift)
    offsets = (req_index * SEG + start_shift).astype(jnp.int32)
    return (offsets, lengths)


def cache_fields(key):
    base_key = jax.random.fold_in(key, 7202)
    key_keys, key_vals, key_mean, key_scale, key_query = jax.random.split(base_key, 5)
    keys_all = jax.random.truncated_normal(key_keys, -4.0, 4.0, (LEN, KVH * HD), jnp.float32)
    channel_mean = jax.random.uniform(key_mean, (1, KVH * HD), jnp.float32, -1.0, 1.0)
    values_all = jax.random.truncated_normal(key_vals, -4.0, 4.0, (LEN, KVH * HD), jnp.float32) + channel_mean
    scales = jnp.exp(jax.random.uniform(key_scale, (2, KVH, LEN), jnp.float32, math.log(0.5), math.log(4.0)))
    queries_all = jax.random.truncated_normal(key_query, -4.0, 4.0, (REQS * SPAN, HEADS * HD), jnp.float32)
    return (keys_all, values_all, scales, queries_all)


def draw_queries(key, part):
    return cache_fields(key)[3].astype(jnp.bfloat16)


def draw_cache(key, part):
    fields = cache_fields(key)
    return jnp.stack([fields[0], fields[1]], 0).astype(jnp.bfloat16)


def draw_cache_scale(key, part):
    return cache_fields(key)[2].astype(jnp.bfloat16)


def draw_offsets(key, part):
    return layout(key)[0]


def draw_lengths(key, part):
    return layout(key)[1]


def levels(own_key, extent, shards, least, largest):
    gain, own = 1.0, jax.random.fold_in(own_key, 6)
    for dim, blocks in shards:
        steps = jnp.exp(jax.random.uniform(jax.random.fold_in(own, dim), (blocks,), jnp.float32, least / len(shards), largest / len(shards)))
        gain = gain * jnp.repeat(steps, extent[dim] // blocks).reshape([-1 if axis == dim else 1 for axis in range(len(extent))])
    return gain


def bell_draw(own_key, shape, scale, most, cuts=(), kind=jnp.bfloat16):
    drawn = scale * jax.random.normal(own_key, shape, jnp.float32)
    if cuts:
        drawn = drawn * levels(own_key, shape, cuts, -0.22, 0.18)
    return jnp.clip(drawn, -most, most).astype(kind)


def setup_inputs(seed: int = 0, part: int = 0) -> dict:
    splits = jax.random.split(jax.random.key(seed), 8)
    part_keys = jax.random.split(jax.random.fold_in(splits[7], part), 8)
    return {
        "queries": draw_queries(jax.random.fold_in(jax.random.fold_in(splits[7], part), 71), part),
        "cache": draw_cache(jax.random.fold_in(jax.random.fold_in(splits[7], part), 71), part),
        "cache_scale": draw_cache_scale(jax.random.fold_in(jax.random.fold_in(splits[7], part), 71), part),
        "offsets": draw_offsets(jax.random.fold_in(jax.random.fold_in(splits[7], part), 71), part),
        "lengths": draw_lengths(jax.random.fold_in(jax.random.fold_in(splits[7], part), 71), part),
        "clamp_code": jax.random.randint(part_keys[5], (1,), 512, 1536).astype(jnp.int32),
        "w_out": bell_draw(splits[6], (HEADS * HD, D), (HEADS * HD) ** -0.5, 0.125, ((0, 16),)),
    }


NEG_FILL = -1e+30

def hadamard(matrix_size):
    counter_index = jnp.arange(matrix_size, dtype=jnp.int32)
    common = counter_index[:, None] & counter_index[None, :]
    parity = jnp.zeros((matrix_size, matrix_size), jnp.int32)
    for bit_place in range(matrix_size.bit_length() - 1):
        parity = parity + (common >> bit_place & 1)
    return jnp.where(parity % 2 == 0, 1.0, -1.0).astype(jnp.float32)

def reference(queries, cache, cache_scale, offsets, lengths, clamp_code, w_out):
    tok_rows = REQS * SPAN
    per_group = HEADS // KVH
    token_ids = jnp.arange(tok_rows, dtype=jnp.int32)
    request = token_ids // SPAN
    within = token_ids % SPAN
    starts = offsets[request]
    last_pos = starts + lengths[request] - SPAN + within
    positions = jnp.arange(LEN, dtype=jnp.int32)
    visible = (positions[None, :] >= starts[:, None]) & (positions[None, :] <= last_pos[:, None])
    inv_root = 1.0 / math.sqrt(HD)

    def one_head(kv_index):
        col_left = (kv_index * HD).astype(jnp.int32)
        key_rows = lax.dynamic_slice_in_dim(cache[0], col_left, HD, 1).astype(jnp.float32)
        value_rows = lax.dynamic_slice_in_dim(cache[1], col_left, HD, 1).astype(jnp.float32)
        query_block = lax.dynamic_slice_in_dim(queries, (kv_index * per_group * HD).astype(jnp.int32), per_group * HD, 1)
        query_block = query_block.reshape(tok_rows, per_group, HD).astype(jnp.float32)
        key_scale = lax.dynamic_index_in_dim(cache_scale[0], kv_index, 0, keepdims=False).astype(jnp.float32)
        value_scale = lax.dynamic_index_in_dim(cache_scale[1], kv_index, 0, keepdims=False).astype(jnp.float32)
        scores = jnp.einsum('tjd,pd->jtp', query_block, key_rows)
        scores = scores * (key_scale * inv_root)[None, None, :]
        masked = jnp.where(visible[None], scores, NEG_FILL)
        row_max = lax.optimization_barrier(jnp.max(masked, axis=2))
        weights = jnp.where(visible[None], jnp.exp(masked - row_max[..., None]), 0.0)
        prob_rows = (weights * value_scale[None, None, :]).astype(jnp.bfloat16)
        numerator = jnp.einsum('jtp,pd->jtd', prob_rows.astype(jnp.float32), value_rows)
        denominator = lax.optimization_barrier(jnp.sum(weights, axis=2))
        return (numerator / denominator[..., None]).astype(jnp.bfloat16)
    attention = lax.map(one_head, jnp.arange(KVH, dtype=jnp.int32)).reshape(HEADS, tok_rows, HD)
    rotated = jnp.einsum('htd,de->hte', attention.astype(jnp.float32), hadamard(HD), precision=lax.Precision.HIGHEST)
    rotated = jnp.einsum('gh,hte->gte', hadamard(HEADS), rotated, precision=lax.Precision.HIGHEST)
    rotated = rotated / math.sqrt(HEADS * HD)
    clip_limit = clamp_code[0].astype(jnp.float32) / 1024.0
    clamped = jnp.clip(rotated, -clip_limit, clip_limit).astype(jnp.bfloat16)
    activation = clamped.transpose(1, 0, 2).reshape(tok_rows, HEADS * HD)
    projected = lax.dot_general(w_out, activation, (((0,), (1,)), ((), ())), preferred_element_type=jnp.float32)
    return projected.astype(jnp.bfloat16)
```

```python
import functools
import math

import jax
import jax.numpy as jnp
from jax import lax
from jax.experimental import pallas as pl
from jax.experimental.pallas import tpu as pltpu
from jax.sharding import PartitionSpec as P

SPAN = 64
LANES = 128
NEG_FILL = -1e30


def hadamard(matrix_size):
    counter_index = jnp.arange(matrix_size, dtype=jnp.int32)
    common = counter_index[:, None] & counter_index[None, :]
    parity = jnp.zeros((matrix_size, matrix_size), jnp.int32)
    for bit_place in range(matrix_size.bit_length() - 1):
        parity = parity + (common >> bit_place & 1)
    return jnp.where(parity % 2 == 0, 1.0, -1.0).astype(jnp.float32)


def masked_scores(query_block, key_rows, key_scale, visible_tile, inv_root):
    scores = jnp.einsum("tjd,pd->jtp", query_block, key_rows, preferred_element_type=jnp.float32)
    scores = scores * (key_scale.astype(jnp.float32) * inv_root)[None, None, :]
    return jnp.where(visible_tile[None], scores, NEG_FILL)


def tile_sums(masked, row_max, visible_tile, value_scale, value_rows):
    weights = jnp.where(visible_tile[None], jnp.exp(masked - row_max[..., None]), 0.0)
    prob_rows = (weights * value_scale.astype(jnp.float32)[None, None, :]).astype(jnp.bfloat16)
    numerator = jnp.einsum("jtp,pd->jtd", prob_rows, value_rows, preferred_element_type=jnp.float32)
    return (numerator, jnp.sum(weights, axis=2))


def general_device(queries, cache, cache_scale, offsets, lengths, clamp_code, w_out):
    my_index = lax.axis_index("head")
    head_dim = queries.shape[1]
    local_len = cache.shape[1]
    kv_count = cache.shape[2] // head_dim
    gathered = lax.all_gather(queries, "head", axis=1, tiled=True)
    tok_rows = gathered.shape[0]
    head_count = gathered.shape[1] // head_dim
    per_group = head_count // kv_count
    token_ids = jnp.arange(tok_rows, dtype=jnp.int32)
    request = token_ids // SPAN
    within = token_ids % SPAN
    req_match = request[:, None] == jnp.arange(offsets.shape[0], dtype=jnp.int32)[None, :]
    starts = jnp.sum(jnp.where(req_match, offsets[None, :], 0), axis=1)
    last_pos = starts + jnp.sum(jnp.where(req_match, lengths[None, :], 0), axis=1) - SPAN + within
    inv_root = 1.0 / math.sqrt(head_dim)
    positions = my_index * local_len + jnp.arange(local_len, dtype=jnp.int32)
    visible = (positions[None, :] >= starts[:, None]) & (positions[None, :] <= last_pos[:, None])
    masked_parts = []
    for kv_index in range(kv_count):
        column_left = kv_index * head_dim
        query_block = gathered[
            :, column_left * per_group : (column_left + head_dim) * per_group
        ].reshape(tok_rows, per_group, head_dim)
        masked_parts.append(
            masked_scores(
                query_block,
                cache[0, :, column_left : column_left + head_dim],
                cache_scale[0, kv_index],
                visible,
                inv_root,
            )
        )
    local_max = jnp.concatenate([jnp.max(masked, axis=2) for masked in masked_parts], 0)
    global_max = lax.pmax(local_max, "head")
    numer_parts = []
    denom_parts = []
    for kv_index in range(kv_count):
        column_left = kv_index * head_dim
        row_max = global_max[kv_index * per_group : (kv_index + 1) * per_group]
        numer_part, denom_part = tile_sums(
            masked_parts[kv_index],
            row_max,
            visible,
            cache_scale[1, kv_index],
            cache[1, :, column_left : column_left + head_dim],
        )
        numer_parts.append(numer_part)
        denom_parts.append(denom_part)
    numerator = jnp.concatenate(numer_parts, 0)
    denominator = jnp.concatenate(denom_parts, 0)
    numer_rows, denom_rows = (
        lax.psum_scatter(numerator, "head", scatter_dimension=1, tiled=True),
        lax.psum_scatter(denominator, "head", scatter_dimension=1, tiled=True),
    )
    token_attention = (numer_rows / denom_rows[..., None]).astype(jnp.bfloat16)
    clip_limit = clamp_code[0].astype(jnp.float32) / 1024.0
    scale_out = 1.0 / math.sqrt(head_count * head_dim)
    hd_matrix = hadamard(head_dim).astype(jnp.bfloat16)
    inner_mixed = jnp.einsum(
        "hrd,de->hre", token_attention, hd_matrix, preferred_element_type=jnp.float32
    )
    rotated = jnp.einsum(
        "gh,hre->gre", hadamard(head_count), inner_mixed, precision=lax.Precision.HIGHEST
    )
    clamped = jnp.clip(rotated * scale_out, -clip_limit, clip_limit).astype(jnp.bfloat16)
    activation = lax.all_to_all(clamped, "head", split_axis=0, concat_axis=1, tiled=True)[0]
    projected = lax.psum_scatter(
        lax.dot_general(
            w_out, activation, (((0,), (1,)), ((), ())), preferred_element_type=jnp.float32
        ),
        "head",
        scatter_dimension=0,
        tiled=True,
    )
    return projected.astype(jnp.bfloat16)


def attend_kernel(pieces, span, inv_root, meta_ref, own_ref, mate_ref, *refs):
    kv_refs = refs[:pieces]
    keep_ref, send_ref, score_ref, query_ref = refs[pieces:]
    local_len = score_ref.shape[2]
    scale_rows = local_len // LANES
    rows = 2 * span
    start, last_first, top_bit = meta_ref[0], meta_ref[1], meta_ref[2]
    query_ref[0:span, :] = own_ref[...]
    query_ref[span:rows, :] = mate_ref[...]
    query = query_ref[...]
    row_id = lax.broadcasted_iota(jnp.int32, (rows, local_len), 0)
    lane_id = lax.broadcasted_iota(jnp.int32, (rows, local_len), 1)
    last = last_first + jnp.where(row_id >= span, row_id - span, row_id)
    highest = jnp.full((rows, local_len), NEG_FILL, jnp.float32)

    def scale_row(kv_ref, which):
        block = kv_ref[2 * local_len : 2 * local_len + 2 * scale_rows, :].astype(jnp.float32)
        parts = [block[which * scale_rows + i : which * scale_rows + i + 1] for i in range(scale_rows)]
        return jnp.concatenate(parts, axis=1)

    for piece, kv_ref in enumerate(kv_refs):
        scores = lax.dot_general(
            query, kv_ref[0:local_len, :], (((1,), (1,)), ((), ())), preferred_element_type=jnp.float32
        )
        scores = scores * (scale_row(kv_ref, 0) * inv_root)
        position = meta_ref[3 + piece] + lane_id
        scores = jnp.where((position >= start) & (position <= last), scores, NEG_FILL)
        score_ref[piece] = scores
        highest = jnp.maximum(highest, scores)
    row_max = jnp.max(highest, axis=1, keepdims=True)
    numerator = jnp.zeros((rows, query.shape[1]), jnp.float32)
    total = jnp.zeros((rows, local_len), jnp.float32)
    for piece, kv_ref in enumerate(kv_refs):
        weights = jnp.exp(score_ref[piece] - row_max)
        total = total + weights
        probs = (weights * scale_row(kv_ref, 1)).astype(jnp.bfloat16)
        numerator = numerator + lax.dot_general(
            probs, kv_ref[local_len : 2 * local_len, :], (((1,), (0,)), ((), ())),
            preferred_element_type=jnp.float32,
        )
    attention = numerator / jnp.sum(total, axis=1, keepdims=True)
    attention = attention.astype(jnp.bfloat16).astype(jnp.float32)
    own, mate = attention[0:span], attention[span:rows]
    sign = (1 - 2 * top_bit).astype(jnp.float32)
    keep_ref[...] = (mate + sign * own).astype(jnp.bfloat16)
    send_ref[...] = (own - sign * mate).astype(jnp.bfloat16)


def project_kernel(pieces, scale_out, sign_ref, mix_ref, *refs):
    u_refs, w_refs = refs[:pieces], refs[pieces : 2 * pieces]
    here_ref, far_ref, side_ref, cross_ref, mixed_ref, act_ref = refs[2 * pieces :]
    tokens, width = u_refs[0].shape
    half_tokens, half_columns = here_ref.shape
    for piece in range(pieces):
        mixed_ref[piece] = (
            jnp.dot(u_refs[piece][...], mix_ref[...], preferred_element_type=jnp.float32)
            * sign_ref[piece]
        )
    step = 32
    for row in range(0, tokens, step):
        limit = sign_ref[2 * pieces + row // half_tokens]
        values = [mixed_ref[piece, row : row + step, :] for piece in range(pieces)]
        bit = 1
        while bit < pieces:
            values = [
                values[i ^ bit] - values[i] if i & bit else values[i] + values[i ^ bit]
                for i in range(pieces)
            ]
            bit *= 2
        for piece in range(pieces):
            clipped = jnp.clip(values[piece] * (sign_ref[pieces + piece] * scale_out), -limit, limit)
            act_ref[row : row + step, piece * width : (piece + 1) * width] = clipped.astype(jnp.bfloat16)
    block = 256
    outs = ((here_ref, far_ref), (side_ref, cross_ref))
    for column in range(0, 2 * half_columns, block):
        sums = jnp.zeros((tokens, block), jnp.float32)
        for piece in range(0, pieces, 2):
            weight = jnp.concatenate(
                [w_refs[piece][:, column : column + block], w_refs[piece + 1][:, column : column + block]],
                axis=0,
            )
            sums = sums + jnp.dot(
                act_ref[:, piece * width : (piece + 2) * width], weight, preferred_element_type=jnp.float32
            )
        side = column // half_columns
        inner = column % half_columns
        for part in range(2):
            out = outs[part][side]
            out[:, inner : inner + block] = sums[
                part * half_tokens : (part + 1) * half_tokens
            ].astype(out.dtype)


def combine_kernel(group_ref, here_ref, far_ref, side_ref, cross_ref, out_ref):
    rows = here_ref.shape[1]
    group = group_ref[0]
    near = here_ref[...] + far_ref[...].astype(jnp.float32)
    other = side_ref[...].astype(jnp.float32) + cross_ref[...].astype(jnp.float32)
    out_ref[pl.ds(pl.multiple_of(group * rows, rows), rows), :] = near.T.astype(jnp.bfloat16)
    out_ref[pl.ds(pl.multiple_of((1 - group) * rows, rows), rows), :] = other.T.astype(jnp.bfloat16)


SMEM = pl.BlockSpec(memory_space=pltpu.SMEM)
VMEM = pl.BlockSpec(memory_space=pltpu.VMEM)


def paired_device(axis_sizes, queries, cache, cache_scale, offsets, lengths, clamp_code, w_out):
    groups, members = axis_sizes
    half = members // 2
    index = lax.axis_index("head")
    group = lax.axis_index("groups")
    top_bit = index // half
    low = index % half
    head_dim = queries.shape[1]
    local_len = cache.shape[1]
    tokens = queries.shape[0]
    span = tokens // 2
    columns = w_out.shape[1] // members
    block = columns // groups

    def hop(value, mask):
        return lax.ppermute(value, "head", [(i, i ^ mask) for i in range(members)])

    def cross(value, mask):
        return lax.ppermute(
            value,
            ("groups", "head"),
            [(g * members + i, (1 - g) * members + (i ^ mask)) for g in range(2) for i in range(members)],
        )

    def spread(value):
        found = [None] * half
        found[0] = value
        for mask in range(2, half, 2):
            found[mask] = hop(value, mask)
        for mask in range(0, half, 2):
            found[mask + 1] = hop(found[mask], 1)
        return found

    packed = jnp.concatenate(
        [cache.reshape(2 * local_len, head_dim), cache_scale.reshape(-1, head_dim)], axis=0
    )
    kv_pieces = spread(packed)
    own_queries = lax.dynamic_slice_in_dim(queries, top_bit * span, span, 0)
    mate_queries = hop(lax.dynamic_slice_in_dim(queries, (1 - top_bit) * span, span, 0), half)

    def weight_for(mask):
        target = low ^ mask
        parts = [
            lax.dynamic_slice_in_dim(w_out, ((top * half + target) * groups + group) * block, block, 1)
            for top in (top_bit, 1 - top_bit)
        ]
        return jnp.concatenate(parts, axis=1)

    weights = [weight_for(0)] + [hop(weight_for(mask), mask) for mask in range(1, half)]

    masks = jnp.arange(half, dtype=jnp.int32)
    start = lax.dynamic_index_in_dim(offsets, top_bit, 0, keepdims=False)
    length = lax.dynamic_index_in_dim(lengths, top_bit, 0, keepdims=False)
    meta = jnp.concatenate(
        [
            jnp.stack([start, start + length - span, top_bit]),
            (top_bit * half + (low ^ masks)) * local_len,
        ]
    ).astype(jnp.int32)
    keep, send = pl.pallas_call(
        functools.partial(attend_kernel, half, span, 1.0 / math.sqrt(head_dim)),
        out_shape=[jax.ShapeDtypeStruct((span, head_dim), jnp.bfloat16)] * 2,
        in_specs=[SMEM] + [VMEM] * (2 + half),
        out_specs=[VMEM] * 2,
        scratch_shapes=[
            pltpu.VMEM((half, tokens, local_len), jnp.float32),
            pltpu.VMEM((tokens, head_dim), jnp.bfloat16),
        ],
        cost_estimate=pl.CostEstimate(
            flops=4 * tokens * half * local_len * head_dim,
            bytes_accessed=4 * half * local_len * head_dim,
            transcendentals=tokens * half * local_len,
        ),
        name="attend",
    )(meta, own_queries, mate_queries, *kv_pieces)

    from_far = hop(send, half)
    from_side = cross(keep, 0)
    from_cross = cross(send, half)
    first = jnp.concatenate([keep, from_far, from_side, from_cross], axis=0)
    second = jnp.concatenate([from_far, keep, from_cross, from_side], axis=0)
    u_pieces = spread(jnp.where(top_bit == 0, first, second))

    def parity(value):
        return sum(value >> bit & 1 for bit in range(half.bit_length() - 1)) % 2

    flips = parity(low & masks)
    signs = jnp.concatenate(
        [
            (1 - 2 * flips).astype(jnp.float32),
            (1 - 2 * ((flips + parity(low)) % 2)).astype(jnp.float32),
            clamp_code.astype(jnp.float32) / 1024.0,
            cross(clamp_code, 0).astype(jnp.float32) / 1024.0,
        ]
    )
    mix = hadamard(head_dim).astype(jnp.bfloat16)
    wide = jax.ShapeDtypeStruct((tokens, block), jnp.float32)
    narrow = jax.ShapeDtypeStruct((tokens, block), jnp.bfloat16)
    here, far, side, crossed = pl.pallas_call(
        functools.partial(project_kernel, half, 1.0 / math.sqrt(members * head_dim)),
        out_shape=[wide, narrow, narrow, narrow],
        in_specs=[SMEM] + [VMEM] * (1 + 2 * half),
        out_specs=[VMEM] * 4,
        scratch_shapes=[
            pltpu.VMEM((half, groups * tokens, head_dim), jnp.float32),
            pltpu.VMEM((groups * tokens, half * head_dim), jnp.bfloat16),
        ],
        cost_estimate=pl.CostEstimate(
            flops=2 * groups * tokens * half * head_dim * 2 * block,
            bytes_accessed=2 * half * head_dim * 2 * block,
            transcendentals=0,
        ),
        name="project",
    )(signs, mix, *u_pieces, *weights)

    got_far = hop(far, half)
    got_side = cross(side, 0)
    got_cross = cross(crossed, half)
    return pl.pallas_call(
        combine_kernel,
        out_shape=jax.ShapeDtypeStruct((columns, tokens), jnp.bfloat16),
        in_specs=[SMEM] + [VMEM] * 4,
        out_specs=VMEM,
        name="combine",
    )(jnp.reshape(group, (1,)).astype(jnp.int32), here, got_far, got_side, got_cross)


def solution(mesh):
    axis_sizes = (mesh.shape["groups"], mesh.shape["head"])

    def per_device(queries, cache, cache_scale, offsets, lengths, clamp_code, w_out):
        members = axis_sizes[1]
        head_dim = queries.shape[1]
        paired = (
            axis_sizes[0] == 2
            and members >= 4
            and members & (members - 1) == 0
            and head_dim == LANES
            and cache.shape[2] == head_dim
            and w_out.shape[0] == head_dim
            and offsets.shape[0] == 2
            and queries.shape[0] == 2 * SPAN
            and cache.shape[1] % LANES == 0
            and w_out.shape[1] % (members * 2 * 256) == 0
        )
        body = functools.partial(paired_device, axis_sizes) if paired else general_device
        return body(queries, cache, cache_scale, offsets, lengths, clamp_code, w_out)

    return jax.shard_map(
        per_device,
        mesh=mesh,
        in_specs=(
            P("groups", "head"),
            P(None, ("groups", "head"), None),
            P(None, None, ("groups", "head")),
            P("groups"),
            P("groups"),
            P("groups"),
            P("head", None),
        ),
        out_specs=P("head", "groups"),
        check_vma=False,
    )
```

```python
import functools
import math

import jax
import jax.numpy as jnp
from jax import lax
from jax.experimental import pallas as pl
from jax.experimental.pallas import tpu as pltpu
from jax.sharding import PartitionSpec as P


SPAN = 64
LANES = 128
NEG_FILL = -1e30


def hadamard(matrix_size):
    counter_index = jnp.arange(matrix_size, dtype=jnp.int32)
    common = counter_index[:, None] & counter_index[None, :]
    parity = jnp.zeros((matrix_size, matrix_size), jnp.int32)
    for bit_place in range(matrix_size.bit_length() - 1):
        parity = parity + (common >> bit_place & 1)
    return jnp.where(parity % 2 == 0, 1.0, -1.0).astype(jnp.float32)


def masked_scores(query_block, key_rows, key_scale, visible_tile, inv_root):
    scores = jnp.einsum("tjd,pd->jtp", query_block, key_rows, preferred_element_type=jnp.float32)
    scores = scores * (key_scale.astype(jnp.float32) * inv_root)[None, None, :]
    return jnp.where(visible_tile[None], scores, NEG_FILL)


def tile_sums(masked, row_max, visible_tile, value_scale, value_rows):
    weights = jnp.where(visible_tile[None], jnp.exp(masked - row_max[..., None]), 0.0)
    prob_rows = (weights * value_scale.astype(jnp.float32)[None, None, :]).astype(jnp.bfloat16)
    numerator = jnp.einsum("jtp,pd->jtd", prob_rows, value_rows, preferred_element_type=jnp.float32)
    return (numerator, jnp.sum(weights, axis=2))


def general_device(queries, cache, cache_scale, offsets, lengths, clamp_code, w_out):
    my_index = lax.axis_index("head")
    head_dim = queries.shape[1]
    local_len = cache.shape[1]
    kv_count = cache.shape[2] // head_dim
    gathered = lax.all_gather(queries, "head", axis=1, tiled=True)
    tok_rows = gathered.shape[0]
    head_count = gathered.shape[1] // head_dim
    per_group = head_count // kv_count
    token_ids = jnp.arange(tok_rows, dtype=jnp.int32)
    request = token_ids // SPAN
    within = token_ids % SPAN
    req_match = request[:, None] == jnp.arange(offsets.shape[0], dtype=jnp.int32)[None, :]
    starts = jnp.sum(jnp.where(req_match, offsets[None, :], 0), axis=1)
    last_pos = starts + jnp.sum(jnp.where(req_match, lengths[None, :], 0), axis=1) - SPAN + within
    inv_root = 1.0 / math.sqrt(head_dim)
    positions = my_index * local_len + jnp.arange(local_len, dtype=jnp.int32)
    visible = (positions[None, :] >= starts[:, None]) & (positions[None, :] <= last_pos[:, None])
    masked_parts = []
    for kv_index in range(kv_count):
        column_left = kv_index * head_dim
        query_block = gathered[
            :, column_left * per_group : (column_left + head_dim) * per_group
        ].reshape(tok_rows, per_group, head_dim)
        masked_parts.append(
            masked_scores(
                query_block,
                cache[0, :, column_left : column_left + head_dim],
                cache_scale[0, kv_index],
                visible,
                inv_root,
            )
        )
    local_max = jnp.concatenate([jnp.max(masked, axis=2) for masked in masked_parts], 0)
    global_max = lax.pmax(local_max, "head")
    numer_parts = []
    denom_parts = []
    for kv_index in range(kv_count):
        column_left = kv_index * head_dim
        row_max = global_max[kv_index * per_group : (kv_index + 1) * per_group]
        numer_part, denom_part = tile_sums(
            masked_parts[kv_index],
            row_max,
            visible,
            cache_scale[1, kv_index],
            cache[1, :, column_left : column_left + head_dim],
        )
        numer_parts.append(numer_part)
        denom_parts.append(denom_part)
    numerator = jnp.concatenate(numer_parts, 0)
    denominator = jnp.concatenate(denom_parts, 0)
    numer_rows, denom_rows = (
        lax.psum_scatter(numerator, "head", scatter_dimension=1, tiled=True),
        lax.psum_scatter(denominator, "head", scatter_dimension=1, tiled=True),
    )
    token_attention = (numer_rows / denom_rows[..., None]).astype(jnp.bfloat16)
    clip_limit = clamp_code[0].astype(jnp.float32) / 1024.0
    scale_out = 1.0 / math.sqrt(head_count * head_dim)
    hd_matrix = hadamard(head_dim).astype(jnp.bfloat16)
    inner_mixed = jnp.einsum(
        "hrd,de->hre", token_attention, hd_matrix, preferred_element_type=jnp.float32
    )
    rotated = jnp.einsum(
        "gh,hre->gre", hadamard(head_count), inner_mixed, precision=lax.Precision.HIGHEST
    )
    clamped = jnp.clip(rotated * scale_out, -clip_limit, clip_limit).astype(jnp.bfloat16)
    activation = lax.all_to_all(clamped, "head", split_axis=0, concat_axis=1, tiled=True)[0]
    projected = lax.psum_scatter(
        lax.dot_general(
            w_out, activation, (((0,), (1,)), ((), ())), preferred_element_type=jnp.float32
        ),
        "head",
        scatter_dimension=0,
        tiled=True,
    )
    return projected.astype(jnp.bfloat16)


def sign_table(size):
    row = lax.broadcasted_iota(jnp.int32, (size, size), 0)
    column = lax.broadcasted_iota(jnp.int32, (size, size), 1)
    return (1 - 2 * parity(row & column, size)).astype(jnp.float32)


def parity(value, size):
    return sum(value >> bit & 1 for bit in range(size.bit_length() - 1)) & 1


def attend_kernel(pieces, span, inv_root, offset_ref, length_ref, own_ref, mate_ref, *refs):
    kv_refs = refs[:pieces]
    keep_ref, send_ref, score_ref, query_ref = refs[pieces:]
    local_len = score_ref.shape[2]
    scale_rows = local_len // LANES
    rows = 2 * span
    index = lax.axis_index("head")
    top_bit = index // pieces
    start = offset_ref[top_bit]
    last_first = start + length_ref[top_bit] - span
    mine = pl.ds(pl.multiple_of(top_bit * span, span), span)
    query_ref[0:span, :] = own_ref[mine, :]
    query_ref[span:rows, :] = mate_ref[mine, :]
    query = query_ref[...]
    row_id = lax.broadcasted_iota(jnp.int32, (rows, local_len), 0)
    lane_id = lax.broadcasted_iota(jnp.int32, (rows, local_len), 1)
    last = last_first + jnp.where(row_id >= span, row_id - span, row_id)
    highest = jnp.full((rows, local_len), NEG_FILL, jnp.float32)

    def scale_row(kv_ref, which):
        block = kv_ref[2 * local_len : 2 * local_len + 2 * scale_rows, :].astype(jnp.float32)
        parts = [block[which * scale_rows + i : which * scale_rows + i + 1] for i in range(scale_rows)]
        return jnp.concatenate(parts, axis=1)

    for piece, kv_ref in enumerate(kv_refs):
        scores = lax.dot_general(
            query, kv_ref[0:local_len, :], (((1,), (1,)), ((), ())), preferred_element_type=jnp.float32
        )
        scores = scores * (scale_row(kv_ref, 0) * inv_root)
        position = (index ^ piece) * local_len + lane_id
        scores = jnp.where((position >= start) & (position <= last), scores, NEG_FILL)
        score_ref[piece] = scores
        highest = jnp.maximum(highest, scores)
    row_max = jnp.max(highest, axis=1, keepdims=True)
    numerator = jnp.zeros((rows, query.shape[1]), jnp.float32)
    total = jnp.zeros((rows, local_len), jnp.float32)
    for piece, kv_ref in enumerate(kv_refs):
        weights = jnp.exp(score_ref[piece] - row_max)
        total = total + weights
        probs = (weights * scale_row(kv_ref, 1)).astype(jnp.bfloat16)
        numerator = numerator + lax.dot_general(
            probs, kv_ref[local_len : 2 * local_len, :], (((1,), (0,)), ((), ())),
            preferred_element_type=jnp.float32,
        )
    attention = numerator / jnp.sum(total, axis=1, keepdims=True)
    attention = attention.astype(jnp.bfloat16).astype(jnp.float32)
    own, mate = attention[0:span], attention[span:rows]
    sign = (1 - 2 * top_bit).astype(jnp.float32)
    keep_ref[...] = (mate + sign * own).astype(jnp.bfloat16)
    send_ref[...] = (own - sign * mate).astype(jnp.bfloat16)


def project_rows(act_ref, w_refs, half_tokens, outs):
    columns = outs[0].shape[1]
    block = min(columns, 256)
    for column in range(0, columns, block):
        weight = jnp.concatenate([w_ref[:, column : column + block] for w_ref in w_refs], axis=0)
        for part, out in enumerate(outs):
            rows = slice(part * half_tokens, (part + 1) * half_tokens)
            sums = jnp.dot(act_ref[rows, :], weight, preferred_element_type=jnp.float32)
            out[:, column : column + block] = sums.astype(out.dtype)


def far_kernel(pieces, scale_out, code_ref, side_code_ref, *refs):
    u_refs, w_refs = refs[:pieces], refs[pieces : 2 * pieces]
    act_ref, far_ref, cross_ref, mixed_ref = refs[2 * pieces :]
    tokens, width = u_refs[0].shape
    half_tokens = far_ref.shape[0]
    low = lax.axis_index("head") % pieces
    mix = sign_table(width).astype(jnp.bfloat16)
    for piece in range(pieces):
        flip = (1 - 2 * parity(low & piece, pieces)).astype(jnp.float32)
        mixed_ref[piece] = (
            jnp.dot(u_refs[piece][...], mix, preferred_element_type=jnp.float32) * flip
        )
    limits = [code_ref[0].astype(jnp.float32) / 1024.0, side_code_ref[0].astype(jnp.float32) / 1024.0]
    scales = [
        (1 - 2 * parity(low ^ (low & piece), pieces)).astype(jnp.float32) * scale_out
        for piece in range(pieces)
    ]
    step = 32
    for row in range(0, tokens, step):
        limit = limits[row // half_tokens]
        values = [mixed_ref[piece, row : row + step, :] for piece in range(pieces)]
        bit = 1
        while bit < pieces:
            values = [
                values[i ^ bit] - values[i] if i & bit else values[i] + values[i ^ bit]
                for i in range(pieces)
            ]
            bit *= 2
        for piece in range(pieces):
            clipped = jnp.clip(values[piece] * scales[piece], -limit, limit)
            act_ref[row : row + step, piece * width : (piece + 1) * width] = clipped.astype(jnp.bfloat16)
    project_rows(act_ref, w_refs, half_tokens, (far_ref, cross_ref))


def near_kernel(pieces, act_ref, *refs):
    here_ref, side_ref = refs[pieces:]
    project_rows(act_ref, refs[:pieces], here_ref.shape[0], (here_ref, side_ref))


def combine_kernel(here_ref, far_ref, side_ref, cross_ref, out_ref):
    rows = here_ref.shape[1]
    group = lax.axis_index("groups")
    near = here_ref[...] + far_ref[...].astype(jnp.float32)
    other = side_ref[...].astype(jnp.float32) + cross_ref[...].astype(jnp.float32)
    out_ref[pl.ds(pl.multiple_of(group * rows, rows), rows), :] = near.T.astype(jnp.bfloat16)
    out_ref[pl.ds(pl.multiple_of((1 - group) * rows, rows), rows), :] = other.T.astype(jnp.bfloat16)


def entry_index(entry, step):
    return (entry, 0, 0)


SMEM = pl.BlockSpec(memory_space=pltpu.SMEM)
VMEM = pl.BlockSpec(memory_space=pltpu.VMEM)


def paired_device(axis_sizes, queries, cache, cache_scale, offsets, lengths, clamp_code, w_out):
    groups, members = axis_sizes
    half = members // 2
    index = lax.axis_index("head")
    group = lax.axis_index("groups")
    top_bit = index // half
    low = index % half
    head_dim = queries.shape[1]
    local_len = cache.shape[1]
    tokens = queries.shape[0]
    span = tokens // 2
    block = w_out.shape[1] // members // groups

    def hop(value, mask):
        return lax.ppermute(value, "head", [(i, i ^ mask) for i in range(members)])

    def cross(value, mask):
        return lax.ppermute(
            value,
            ("groups", "head"),
            [(g * members + i, (1 - g) * members + (i ^ mask)) for g in range(2) for i in range(members)],
        )

    def spread(value):
        found = [None] * half
        found[0] = value
        for mask in range(half - 2, 0, -2):
            found[mask] = hop(value, mask)
        for mask in range(0, half, 2):
            found[mask + 1] = hop(found[mask], 1)
        return found

    packed = jnp.concatenate(
        [cache.reshape(2 * local_len, head_dim), cache_scale.reshape(-1, head_dim)], axis=0
    )
    kv_pieces = spread(packed)
    mate_queries = hop(queries, half)
    side_code = cross(clamp_code, 0)

    def weights_for(source, top):
        pairs = []
        for mask in range(0, half, 2):
            parts = []
            for near in (mask, mask + 1):
                start = ((top * half + (low ^ near)) * groups + group) * block
                parts.append(lax.dynamic_slice_in_dim(source, start, block, 1))
            pair = jnp.stack(parts)
            pairs.append(hop(pair, mask) if mask else pair)
        found = []
        for mask, pair in zip(range(0, half, 2), pairs):
            found += [pair, hop(pair, 1)]
        return found

    far_weights = weights_for(w_out, 1 - top_bit)

    keep, send = pl.pallas_call(
        functools.partial(attend_kernel, half, span, 1.0 / math.sqrt(head_dim)),
        out_shape=[jax.ShapeDtypeStruct((span, head_dim), jnp.bfloat16)] * 2,
        in_specs=[SMEM] * 2 + [VMEM] * (2 + half),
        out_specs=[VMEM] * 2,
        scratch_shapes=[
            pltpu.VMEM((half, tokens, local_len), jnp.float32),
            pltpu.VMEM((tokens, head_dim), jnp.bfloat16),
        ],
        cost_estimate=pl.CostEstimate(
            flops=4 * tokens * half * local_len * head_dim,
            bytes_accessed=4 * half * local_len * head_dim,
            transcendentals=tokens * half * local_len,
        ),
        name="attend",
    )(offsets, lengths, queries, mate_queries, *kv_pieces)

    from_far = hop(send, half)
    from_cross = cross(send, half)
    from_side = cross(keep, 0)
    first = jnp.concatenate([keep, from_far, from_side, from_cross], axis=0)
    second = jnp.concatenate([from_far, keep, from_cross, from_side], axis=0)
    u_pieces = spread(jnp.where(top_bit == 0, first, second))
    near_weights = weights_for(w_out, top_bit)
    pair_specs = [
        pl.BlockSpec((None, head_dim, block), functools.partial(entry_index, mask & 1)) for mask in range(half)
    ]

    wide = jax.ShapeDtypeStruct((tokens, block), jnp.float32)
    narrow = jax.ShapeDtypeStruct((tokens, block), jnp.bfloat16)
    flat = jax.ShapeDtypeStruct((groups * tokens, half * head_dim), jnp.bfloat16)
    cost = pl.CostEstimate(
        flops=2 * groups * tokens * half * head_dim * block,
        bytes_accessed=2 * half * head_dim * block,
        transcendentals=0,
    )
    act, far, crossed = pl.pallas_call(
        functools.partial(far_kernel, half, 1.0 / math.sqrt(members * head_dim)),
        out_shape=[flat, narrow, narrow],
        grid=(1,),
        in_specs=[SMEM] * 2 + [VMEM] * half + pair_specs,
        out_specs=[VMEM] * 3,
        scratch_shapes=[pltpu.VMEM((half, groups * tokens, head_dim), jnp.float32)],
        cost_estimate=cost,
        name="far",
    )(clamp_code, side_code, *u_pieces, *far_weights)
    got_far = hop(far, half)
    got_cross = cross(crossed, half)
    here, side = pl.pallas_call(
        functools.partial(near_kernel, half),
        out_shape=[wide, narrow],
        grid=(1,),
        in_specs=[VMEM] + pair_specs,
        out_specs=[VMEM] * 2,
        cost_estimate=cost,
        name="near",
    )(act, *near_weights)
    got_side = cross(side, 0)
    return pl.pallas_call(
        combine_kernel,
        out_shape=jax.ShapeDtypeStruct((groups * block, tokens), jnp.bfloat16),
        in_specs=[VMEM] * 4,
        out_specs=VMEM,
        name="combine",
    )(here, got_far, got_side, got_cross)


def solution(mesh):
    axis_sizes = (mesh.shape["groups"], mesh.shape["head"])

    def per_device(queries, cache, cache_scale, offsets, lengths, clamp_code, w_out):
        members = axis_sizes[1]
        head_dim = queries.shape[1]
        paired = (
            axis_sizes[0] == 2
            and members >= 4
            and members & (members - 1) == 0
            and head_dim == LANES
            and cache.shape[2] == head_dim
            and w_out.shape[0] == head_dim
            and offsets.shape[0] == 2
            and queries.shape[0] == 2 * SPAN
            and cache.shape[1] % LANES == 0
            and w_out.shape[1] % (members * 2 * 256) == 0
        )
        if not paired:
            return general_device(queries, cache, cache_scale, offsets, lengths, clamp_code, w_out)
        return paired_device(
            axis_sizes, queries, cache, cache_scale, offsets, lengths, clamp_code, w_out
        )

    return jax.shard_map(
        per_device,
        mesh=mesh,
        in_specs=(
            P("groups", "head"),
            P(None, ("groups", "head"), None),
            P(None, None, ("groups", "head")),
            P("groups"),
            P("groups"),
            P("groups"),
            P("head", None),
        ),
        out_specs=P("head", "groups"),
        check_vma=False,
    )
```
